32 devices in a mesh: grp: 2 (over x), tok: 4 (over z), head: 4 (over y, core).
Axes of the slice: x: 2, y: 2, z: 4, core: 2. Of those that a mesh axis runs over, the one named last changes fastest.
Arguments:
- views: bfloat16 [2, 2, 768, 1024], P('grp', None, 'tok'), may hold values from -6 to 6
- q_weight: bfloat16 [1024, 1024], P(None, 'head'), may hold values from -0.1875 to 0.1875
- k_weight: bfloat16 [1024, 1024], P(None, 'head'), may hold values from -0.1875 to 0.1875
- v_weight: bfloat16 [1024, 1024], P(None, 'head'), may hold values from -0.1875 to 0.1875
- rate_weight: bfloat16 [1024, 4], P(None, 'head'), may hold values from -0.1875 to 0.1875
- fast_in: float32 [4, 256, 1024], P('head', None, 'tok'), may hold values from -0.375 to 0.375
- fast_out: float32 [4, 512, 256], P('head', None, 'tok'), may hold values from -0.25 to 0.25
- out_gain: float32 [1024], P('head'), may hold values from 0.1 to 1.9
Outputs:
- rendered: bfloat16 [2, 2, 768, 1024], P('grp', None, 'tok', 'head')
The draws below stay inside these ranges and needn't reach their ends.
All inputs are finite; a program needn't handle non-finite values.
Results may differ from the reference program's by a relative error of at most 0.013.
Values may be sent and summed in bfloat16 or wider, within the bound.
A program may use at most 64 MiB of HBM per device.

```python
import math
import jax
import jax.numpy as jnp
from jax import lax

D = 1024
H = 4
DH = 256
HF = 512
SPANS = 2
TOKENS = 768


def shard_levels(rng, extent, split, smallest, largest):
    factor_of, own = 1.0, jax.random.fold_in(rng, 6)
    for axis_at, blocks in split:
        draws = jnp.exp(jax.random.uniform(jax.random.fold_in(own, axis_at), (blocks,), jnp.float32, smallest / len(split), largest / len(split)))
        factor_of = factor_of * jnp.repeat(draws, extent[axis_at] // blocks).reshape([-1 if axis == axis_at else 1 for axis in range(len(extent))])
    return factor_of


def gaussian(stream_key, dims, deviation, most, cuts=(), dtype=jnp.bfloat16):
    drawn = deviation * jax.random.normal(stream_key, dims, jnp.float32)
    if cuts:
        drawn = drawn * shard_levels(stream_key, dims, cuts, -0.22, 0.18)
    return jnp.clip(drawn, -most, most).astype(dtype)


def setup_inputs(seed: int = 0) -> dict:
    key_list = jax.random.split(jax.random.key(seed), 9)
    return {
        "views": gaussian(key_list[0], (2, SPANS, TOKENS, D), 1.0, 6.0, ((0, 2), (2, 4))),
        "q_weight": gaussian(key_list[1], (D, D), D ** -0.5, 0.1875, ((1, 4),)),
        "k_weight": gaussian(key_list[2], (D, D), D ** -0.5, 0.1875, ((1, 4),)),
        "v_weight": gaussian(key_list[3], (D, D), D ** -0.5, 0.1875, ((1, 4),)),
        "rate_weight": gaussian(key_list[4], (D, H), D ** -0.5, 0.1875, ((1, 4),)),
        "fast_in": gaussian(key_list[5], (H, DH, 2 * HF), DH ** -0.5, 0.375, ((0, 4), (2, 4)), jnp.float32),
        "fast_out": gaussian(key_list[6], (H, HF, DH), HF ** -0.5, 0.25, ((0, 4), (2, 4)), jnp.float32),
        "out_gain": jnp.clip(1.0 + 0.18 * jax.random.normal(key_list[7], (D,), jnp.float32), 0.1, 1.9),
    }


norm_eps = 1e-06
out_eps = 1e-05
step_coef = 0.3
momentum_keep = 0.5

def rms_scale(values):
    return values * lax.rsqrt(lax.optimization_barrier(jnp.mean(values * values, axis=-1, keepdims=True)) + norm_eps)

def contract_rows(left, right):
    return lax.dot_general(left, right, (((0,), (0,)), ((), ())), preferred_element_type=jnp.float32)

def contract_cols(left, right):
    return lax.dot_general(left, right, (((1,), (1,)), ((), ())), preferred_element_type=jnp.float32)

def fast_grads(inputs, key_proj, value_proj, rate_proj, copy_in, copy_out, step_size):
    hidden_units = copy_out.shape[0]
    keyed = rms_scale(jnp.dot(inputs, key_proj, preferred_element_type=jnp.float32)).astype(jnp.bfloat16)
    valued = jnp.dot(inputs, value_proj, preferred_element_type=jnp.float32)
    rates = jax.nn.softplus(jnp.dot(inputs, rate_proj, preferred_element_type=jnp.float32))
    upstream = (-(step_size * rates) * valued).astype(jnp.bfloat16)
    pre_act = jnp.dot(keyed, copy_in, preferred_element_type=jnp.float32)
    gate = pre_act[:, :hidden_units]
    upper = pre_act[:, hidden_units:]
    sigma = jax.nn.sigmoid(gate)
    active = gate * sigma
    hidden = (active * upper).astype(jnp.bfloat16)
    grad_out = contract_rows(hidden, upstream)
    back = contract_cols(upstream, copy_out)
    back_pre = jnp.concatenate([back * upper * sigma * (1.0 + gate * (1.0 - sigma)), back * active], axis=1).astype(jnp.bfloat16)
    grad_in = contract_rows(keyed, back_pre)
    return (grad_in, grad_out)

def fast_apply(queries, copy_in, copy_out):
    hidden_units = copy_out.shape[0]
    pre_act = jnp.dot(queries, copy_in, preferred_element_type=jnp.float32)
    gate = pre_act[:, :hidden_units]
    upper = pre_act[:, hidden_units:]
    hidden = (gate * jax.nn.sigmoid(gate) * upper).astype(jnp.bfloat16)
    return jnp.dot(hidden, copy_out, preferred_element_type=jnp.float32)

def renormalize(trial, base_squares):
    return trial * jnp.sqrt(base_squares) * lax.rsqrt(lax.optimization_barrier(jnp.mean(trial * trial, axis=0, keepdims=True)) + norm_eps)

def reference(views, q_weight, k_weight, v_weight, rate_weight, fast_in, fast_out, out_gain):
    spans = views.shape[1]
    heads = fast_in.shape[0]
    head_size = fast_in.shape[1]
    step_size = step_coef / math.sqrt(views.shape[2])
    state_in = [fast_in[h] for h in range(heads)]
    state_out = [fast_out[h] for h in range(heads)]
    base_in = [lax.optimization_barrier(jnp.mean(fast_in[h] * fast_in[h], axis=0, keepdims=True)) for h in range(heads)]
    base_out = [lax.optimization_barrier(jnp.mean(fast_out[h] * fast_out[h], axis=0, keepdims=True)) for h in range(heads)]
    moment_in = [jnp.zeros_like(fast_in[h]) for h in range(heads)]
    moment_out = [jnp.zeros_like(fast_out[h]) for h in range(heads)]
    copies_in = [state_in[h].astype(jnp.bfloat16) for h in range(heads)]
    copies_out = [state_out[h].astype(jnp.bfloat16) for h in range(heads)]
    groups = [[], []]
    for span in range(spans):
        inputs = views[0, span]
        for h in range(heads):
            cols = slice(h * head_size, (h + 1) * head_size)
            grad_in, grad_out = fast_grads(inputs, k_weight[:, cols], v_weight[:, cols], rate_weight[:, h:h + 1], copies_in[h], copies_out[h], step_size)
            moment_in[h] = momentum_keep * moment_in[h] + grad_in
            moment_out[h] = momentum_keep * moment_out[h] + grad_out
            state_in[h] = renormalize(state_in[h] - moment_in[h], base_in[h])
            state_out[h] = renormalize(state_out[h] - moment_out[h], base_out[h])
            copies_in[h] = state_in[h].astype(jnp.bfloat16)
            copies_out[h] = state_out[h].astype(jnp.bfloat16)
        for group in range(2):
            pieces = []
            for h in range(heads):
                cols = slice(h * head_size, (h + 1) * head_size)
                queries = rms_scale(jnp.dot(views[group, span], q_weight[:, cols], preferred_element_type=jnp.float32)).astype(jnp.bfloat16)
                pieces.append(fast_apply(queries, copies_in[h], copies_out[h]))
            joined = jnp.concatenate(pieces, axis=1)
            normed = joined * lax.rsqrt(lax.optimization_barrier(jnp.mean(joined * joined, axis=1, keepdims=True)) + out_eps) * out_gain
            groups[group].append(normed.astype(jnp.bfloat16))
    return jnp.stack([jnp.stack(groups[0]), jnp.stack(groups[1])])
```

```python
import functools
import math

import jax
import jax.numpy as jnp
from jax import lax
from jax.experimental import pallas as pl
from jax.experimental.pallas import tpu as pltpu
from jax.sharding import PartitionSpec as P

norm_eps = 1e-06
out_eps = 1e-05
step_coef = 0.3
momentum_keep = 0.5


def spread(value, axis, source):
    kept = jnp.where(lax.axis_index(axis) == source, value, 0).astype(value.dtype)
    return lax.psum(kept, axis)


def rms_scale(values):
    return values * lax.rsqrt(jnp.mean(values * values, axis=-1, keepdims=True) + norm_eps)


def contract_rows(left, right):
    return lax.dot_general(
        left, right, (((0,), (0,)), ((), ())), preferred_element_type=jnp.float32
    )


def contract_cols(left, right):
    return lax.dot_general(
        left, right, (((1,), (1,)), ((), ())), preferred_element_type=jnp.float32
    )


def fast_apply(queries, copy_in, copy_out):
    hidden_units = copy_out.shape[0]
    pre_act = jnp.dot(queries, copy_in, preferred_element_type=jnp.float32)
    gate = pre_act[:, :hidden_units]
    upper = pre_act[:, hidden_units:]
    hidden = (gate * jax.nn.sigmoid(gate) * upper).astype(jnp.bfloat16)
    return jnp.dot(hidden, copy_out, preferred_element_type=jnp.float32)


def by_collectives(views, q_weight, k_weight, v_weight, rate_weight, fast_in, fast_out, out_gain):
    tok_count = lax.axis_size("tok")
    is_input = lax.axis_index("grp") == 0
    spans = views.shape[1]
    head_size = fast_in.shape[1]
    hidden_units = fast_out.shape[1]
    step_size = step_coef / math.sqrt(views.shape[2] * tok_count)
    width_all = head_size * lax.axis_size("head")
    whole_in, whole_out = (
        lax.all_gather(fast_in, "tok", axis=2, tiled=True),
        lax.all_gather(fast_out, "tok", axis=2, tiled=True),
    )
    whole_in = whole_in[0]
    whole_out = whole_out[0]
    copy_in = whole_in.astype(jnp.bfloat16)
    copy_out = whole_out.astype(jnp.bfloat16)
    state_in = fast_in[0]
    state_out = fast_out[0]
    base_in = jnp.mean(state_in * state_in, axis=0, keepdims=True)
    base_out = jnp.mean(state_out * state_out, axis=0, keepdims=True)
    moment_in = jnp.zeros_like(state_in)
    moment_out = jnp.zeros_like(state_out)

    def input_grads(inputs, given_in, given_out):
        keyed = rms_scale(jnp.dot(inputs, k_weight, preferred_element_type=jnp.float32)).astype(
            jnp.bfloat16
        )
        valued = jnp.dot(inputs, v_weight, preferred_element_type=jnp.float32)
        rates = jax.nn.softplus(jnp.dot(inputs, rate_weight, preferred_element_type=jnp.float32))
        upstream = (-(step_size * rates) * valued).astype(jnp.bfloat16)
        pre_act = jnp.dot(keyed, given_in, preferred_element_type=jnp.float32)
        gate = pre_act[:, :hidden_units]
        upper = pre_act[:, hidden_units:]
        sigma = jax.nn.sigmoid(gate)
        active = gate * sigma
        hidden = (active * upper).astype(jnp.bfloat16)
        grad_out = contract_rows(hidden, upstream)
        back = contract_cols(upstream, given_out)
        back_pre = jnp.concatenate(
            [back * upper * sigma * (1.0 + gate * (1.0 - sigma)), back * active], axis=1
        ).astype(jnp.bfloat16)
        grad_in = contract_rows(keyed, back_pre)
        return (grad_in, grad_out)

    def novel_grads(inputs, given_in, given_out):
        return (
            jnp.zeros((head_size, 2 * hidden_units), jnp.float32),
            jnp.zeros((hidden_units, head_size), jnp.float32),
        )

    outputs = []
    for span in range(spans):
        inputs = views[0, span]
        queries = rms_scale(jnp.dot(inputs, q_weight, preferred_element_type=jnp.float32)).astype(
            jnp.bfloat16
        )
        grads = lax.cond(is_input, input_grads, novel_grads, inputs, copy_in, copy_out)
        grad_in, grad_out = lax.psum_scatter(grads, "tok", scatter_dimension=1, tiled=True)
        moment_in = momentum_keep * moment_in + grad_in
        moment_out = momentum_keep * moment_out + grad_out
        trial_in = state_in - moment_in
        trial_out = state_out - moment_out
        mean_in = jnp.mean(trial_in * trial_in, axis=0, keepdims=True)
        mean_out = jnp.mean(trial_out * trial_out, axis=0, keepdims=True)
        state_in = trial_in * jnp.sqrt(base_in) * lax.rsqrt(mean_in + norm_eps)
        state_out = trial_out * jnp.sqrt(base_out) * lax.rsqrt(mean_out + norm_eps)
        part_in = state_in.astype(jnp.bfloat16)
        part_out = state_out.astype(jnp.bfloat16)
        copy_in, copy_out = (
            lax.all_gather(part_in, "tok", axis=1, tiled=True),
            lax.all_gather(part_out, "tok", axis=1, tiled=True),
        )
        copy_in, copy_out = (spread(copy_in, "grp", 0), spread(copy_out, "grp", 0))
        produced = fast_apply(queries, copy_in, copy_out)
        squares = lax.psum(jnp.sum(produced * produced, axis=1), "head")
        normed = produced * lax.rsqrt(squares / width_all + out_eps)[:, None] * out_gain
        outputs.append(normed.astype(jnp.bfloat16))
    return jnp.stack(outputs)[None]


def fused_kernel(
    tok_count, grp_count, head_count,
    views_ref, q_ref, k_ref, v_ref, rate_ref, in_ref, out_ref, gain_ref,
    res_ref,
    pieces, packed, queries, moment_in, moment_out, state_in, state_out, copy_in, copy_out,
    base_in, base_out, produced, squares,
    local_sem,
    first_send, first_recv, z_send, z_recv, x_send, x_recv, y_send, y_recv,
    c1_send, c1_recv, c2_send, c2_recv, wz_send, wz_recv, wx_send, wx_recv, sq_send, sq_recv,
):
    tok, grp, head = lax.axis_index("tok"), lax.axis_index("grp"), lax.axis_index("head")
    spans, rows, width = views_ref.shape[1:]
    piece = pieces.shape[-1]
    head_size, block_in = in_ref.shape[1:]
    hidden_units, block_out = out_ref.shape[1:]
    pack = packed.shape[-1] - block_in
    folds = pack // block_out
    half = head_size // grp_count
    step_size = step_coef / math.sqrt(rows * tok_count)
    other_grp = {"grp": 1 - grp}
    far_bit = head_count // 2
    far_head = jnp.where(head < far_bit, head + far_bit, head - far_bit)
    flip = 1 - 2 * lax.rem(head, 2)
    near_head = head + flip
    far = {"head": far_head}
    near = {"head": near_head}

    def shard(step):
        return lax.rem(tok - step + tok_count, tok_count)

    def peer(step):
        return {"tok": lax.rem(tok + step, tok_count)}

    def remote(src, dst, send, recv, target):
        return pltpu.make_async_remote_copy(
            src_ref=src, dst_ref=dst, send_sem=send, recv_sem=recv,
            device_id=target, device_id_type=pl.DeviceIdType.MESH,
        )

    def view_piece(span, part):
        start = pl.multiple_of((head * grp_count + part) * piece, piece)
        return views_ref.at[0, span, :, pl.ds(start, piece)]

    def same(ref, send, recv, target):
        return remote(ref, ref, send, recv, target)

    own = [
        pltpu.make_async_copy(view_piece(s, 0), pieces.at[s, tok, head, 0], local_sem.at[s])
        for s in range(spans)
    ]
    first = [
        remote(view_piece(s, 1), pieces.at[s, tok, head, 1], first_send.at[s], first_recv.at[s], other_grp)
        for s in range(spans)
    ]
    along_z = [
        [
            same(pieces.at[s, tok, head, grp], z_send.at[s, d], z_recv.at[s, d], peer(d + 1))
            for d in range(tok_count - 1)
        ]
        for s in range(spans)
    ]
    along_x = [
        [
            same(pieces.at[s, shard(d), head, grp], x_send.at[s, d], x_recv.at[s, d], other_grp)
            for d in range(tok_count)
        ]
        for s in range(spans)
    ]
    along_y = [
        [
            same(pieces.at[s, shard(d), head], y_send.at[s, d], y_recv.at[s, d], far)
            for d in range(tok_count)
        ]
        for s in range(spans)
    ]
    core_own = [
        [
            same(pieces.at[s, shard(d), head], c1_send.at[s, d], c1_recv.at[s, d], near)
            for d in range(tok_count)
        ]
        for s in range(spans)
    ]
    core_far = [
        [
            same(pieces.at[s, shard(d), far_head], c2_send.at[s, d], c2_recv.at[s, d], near)
            for d in range(tok_count)
        ]
        for s in range(spans)
    ]
    my_half = pl.ds(pl.multiple_of(grp * half, half), half)
    fast_z = [
        same(packed.at[tok, my_half], wz_send.at[d], wz_recv.at[d], peer(d + 1))
        for d in range(tok_count - 1)
    ]
    fast_x = [
        same(packed.at[shard(d + 1), my_half], wx_send.at[d], wx_recv.at[d], other_grp)
        for d in range(tok_count - 1)
    ]
    square = [
        [
            same(squares.at[s, head], sq_send.at[s, d], sq_recv.at[s, d],
                 {"head": lax.rem(head + d + 1, head_count)})
            for d in range(head_count - 1)
        ]
        for s in range(spans)
    ]

    barrier = pltpu.get_barrier_semaphore()
    partners = [peer(d + 1) for d in range(tok_count - 1)] + [other_grp]
    partners += [{"head": lax.rem(head + d + 1, head_count)} for d in range(head_count - 1)]
    for target in partners:
        pl.semaphore_signal(barrier, inc=1, device_id=target, device_id_type=pl.DeviceIdType.MESH)

    @pl.when(grp == 0)
    def _():
        for copy in own:
            copy.start()

    packed[tok, :, :block_in] = in_ref[0].astype(jnp.bfloat16)
    fold_rows = hidden_units // folds
    packed[tok, :, block_in:] = jnp.concatenate(
        [out_ref[0, f * fold_rows:(f + 1) * fold_rows, :] for f in range(folds)], axis=1
    ).astype(jnp.bfloat16)
    pl.semaphore_wait(barrier, len(partners))

    @pl.when(grp == 0)
    def _():
        for s in range(spans):
            first[s].start()
        for copy in own:
            copy.wait()
        for copy in along_z[0]:
            copy.start()

    for copy in fast_z:
        copy.start()

    @pl.when(grp == 1)
    def _():
        first[0].wait_recv()
        for copy in along_z[0]:
            copy.start()

    along_x[0][0].start()

    @pl.when(grp == 1)
    def _():
        first[1].wait_recv()

    for s in range(1, spans):
        for copy in along_z[s]:
            copy.start()
    for s in range(spans):
        queries[s] = rms_scale(
            jnp.dot(views_ref[0, s], q_ref[...], preferred_element_type=jnp.float32)
        ).astype(jnp.bfloat16)
    for d in range(tok_count - 1):
        along_z[0][d].wait_recv()
        along_x[0][d + 1].start()
    for d in range(tok_count - 1):
        fast_z[d].wait_recv()
        fast_x[d].start()
    along_x[1][0].start()
    for d in range(tok_count):
        along_x[0][d].wait_recv()
        along_y[0][d].start()
        core_own[0][d].start()
    for d in range(tok_count - 1):
        along_z[1][d].wait_recv()
        along_x[1][d + 1].start()
    for d in range(tok_count):
        along_y[0][d].wait_recv()
        core_far[0][d].start()
    for d in range(tok_count):
        along_x[1][d].wait_recv()
        along_y[1][d].start()
        core_own[1][d].start()
    for d in range(tok_count - 1):
        fast_x[d].wait_recv()

    for t in range(tok_count):
        cols = slice(t * block_in, (t + 1) * block_in)
        given = packed[t, :, :block_in]
        wide = given.astype(jnp.float32)
        copy_in[:, cols] = given
        state_in[:, cols] = wide
        base_in[:, cols] = jnp.sqrt(jnp.mean(wide * wide, axis=0, keepdims=True))
    for f in range(folds):
        given = jnp.concatenate(
            [packed[t, :, block_in + f * block_out:block_in + (f + 1) * block_out].astype(jnp.float32)
             for t in range(tok_count)], axis=1
        )
        copy_out[f * fold_rows:(f + 1) * fold_rows, :] = given.astype(jnp.bfloat16)
        state_out[f * fold_rows:(f + 1) * fold_rows, :] = given
    base_out[...] = jnp.sqrt(jnp.mean(state_out[...] * state_out[...], axis=0, keepdims=True))
    moment_in[...] = jnp.zeros_like(moment_in)
    moment_out[...] = jnp.zeros_like(moment_out)

    def add_grads(span, t):
        inputs = jnp.concatenate(
            [pieces[span, t, h, g] for h in range(head_count) for g in range(grp_count)], axis=1
        )
        keyed = rms_scale(jnp.dot(inputs, k_ref[...], preferred_element_type=jnp.float32)).astype(
            jnp.bfloat16
        )
        valued = jnp.dot(inputs, v_ref[...], preferred_element_type=jnp.float32)
        raw = jnp.dot(inputs, rate_ref[...], preferred_element_type=jnp.float32)[:, :1]
        rates = jnp.maximum(raw, 0.0) + jnp.log1p(jnp.exp(-jnp.abs(raw)))
        upstream = (-(step_size * rates) * valued).astype(jnp.bfloat16)
        gate = jnp.dot(keyed, copy_in[:, :hidden_units], preferred_element_type=jnp.float32)
        upper = jnp.dot(keyed, copy_in[:, hidden_units:], preferred_element_type=jnp.float32)
        sigma = jax.nn.sigmoid(gate)
        active = gate * sigma
        hidden = (active * upper).astype(jnp.bfloat16)
        moment_out[...] += contract_rows(hidden, upstream)
        back = contract_cols(upstream, copy_out[...])
        back_gate = (back * upper * sigma * (1.0 + gate * (1.0 - sigma))).astype(jnp.bfloat16)
        back_upper = (back * active).astype(jnp.bfloat16)
        moment_in[:, :hidden_units] += contract_rows(keyed, back_gate)
        moment_in[:, hidden_units:] += contract_rows(keyed, back_upper)

    def renormalize(state, moment, base, copy, cols):
        trial = state[:, cols] - moment[:, cols]
        mean = jnp.mean(trial * trial, axis=0, keepdims=True)
        state[:, cols] = trial * base[:, cols] * lax.rsqrt(mean + norm_eps)
        copy[:, cols] = state[:, cols].astype(jnp.bfloat16)
        moment[:, cols] = moment[:, cols] * momentum_keep

    for s in range(spans):
        for d in range(tok_count):
            core_own[s][d].wait_recv()
            core_far[s][d].wait_recv()
        lax.fori_loop(0, tok_count, lambda t, c: (add_grads(s, t), c)[1], 0)
        if s + 1 < spans:
            for d in range(tok_count):
                along_y[s + 1][d].wait_recv()
                core_far[s + 1][d].start()
        for t in range(tok_count):
            renormalize(state_in, moment_in, base_in, copy_in, slice(t * block_in, (t + 1) * block_in))
        renormalize(state_out, moment_out, base_out, copy_out, slice(None))
        made = fast_apply(queries[s], copy_in[...], copy_out[...])
        produced[s] = made
        sums = jnp.sum(made * made, axis=1, keepdims=True)
        squares[s, head] = jnp.transpose(jnp.broadcast_to(sums, (rows, 128)))[:8]
        for copy in square[s]:
            copy.start()

    for s in range(spans):
        for copy in square[s]:
            copy.wait_recv()
        total = squares[s, 0]
        for h in range(1, head_count):
            total = total + squares[s, h]
        scale = lax.rsqrt(total / (head_size * head_count) + out_eps)
        column = jnp.transpose(jnp.concatenate([scale] * 16, axis=0))[:, :1]
        res_ref[0, s] = (produced[s] * column * gain_ref[...]).astype(jnp.bfloat16)

    @pl.when(grp == 0)
    def _():
        for copy in first:
            copy.wait_send()

    for group in (along_z, along_x, along_y, core_own, core_far, square):
        for copies in group:
            for copy in copies:
                copy.wait_send()
    for copy in fast_z + fast_x:
        copy.wait_send()


def by_kernel(sizes, views, q_weight, k_weight, v_weight, rate_weight, fast_in, fast_out, out_gain):
    tok_count, grp_count, head_count = sizes
    _, spans, rows, width = views.shape
    _, head_size, block_in = fast_in.shape
    _, hidden_units, block_out = fast_out.shape
    piece = width // (grp_count * head_count)
    pack = block_out * (hidden_units // head_size)
    dma = pltpu.SemaphoreType.DMA
    vmem = pltpu.VMEM
    pair = [dma((spans, tok_count))] * 2
    return pl.pallas_call(
        functools.partial(fused_kernel, tok_count, grp_count, head_count),
        out_shape=jax.ShapeDtypeStruct((1, spans, rows, head_size), jnp.bfloat16),
        in_specs=[pl.BlockSpec(memory_space=pltpu.VMEM)] * 8,
        out_specs=pl.BlockSpec(memory_space=pltpu.VMEM),
        scratch_shapes=[
            vmem((spans, tok_count, head_count, grp_count, rows, piece), jnp.bfloat16),
            vmem((tok_count, head_size, block_in + pack), jnp.bfloat16),
            vmem((spans, rows, head_size), jnp.bfloat16),
            vmem((head_size, 2 * hidden_units), jnp.float32),
            vmem((hidden_units, head_size), jnp.float32),
            vmem((head_size, 2 * hidden_units), jnp.float32),
            vmem((hidden_units, head_size), jnp.float32),
            vmem((head_size, 2 * hidden_units), jnp.bfloat16),
            vmem((hidden_units, head_size), jnp.bfloat16),
            vmem((1, 2 * hidden_units), jnp.float32),
            vmem((1, head_size), jnp.float32),
            vmem((spans, rows, head_size), jnp.float32),
            vmem((spans, head_count, 8, rows), jnp.float32),
            dma((spans,)),
            *[dma((spans,))] * 2,
            *[dma((spans, tok_count - 1))] * 2,
            *pair, *pair, *pair, *pair,
            *[dma((tok_count - 1,))] * 4,
            *[dma((spans, head_count - 1))] * 2,
        ],
        compiler_params=pltpu.CompilerParams(collective_id=0, has_side_effects=True),
        name="fused_layer",
    )(views, q_weight, k_weight, v_weight, rate_weight, fast_in, fast_out, out_gain.reshape(1, -1))


def local(sizes, views, *rest):
    tok_count, grp_count, head_count = sizes
    fast_in, fast_out = rest[4], rest[5]
    head_size, hidden_units = fast_in.shape[1], fast_out.shape[1]
    piece = views.shape[3] // (grp_count * head_count)
    few = tok_count * views.shape[2] <= 4 * head_size
    fits = (
        tok_count > 1 and grp_count == 2 and head_count == 4 and piece % 128 == 0
        and fast_in.shape[2] % 128 == 0 and views.shape[2] % 16 == 0 and hidden_units % head_size == 0
        and fast_out.shape[2] * (hidden_units // head_size) % 128 == 0
    )
    if few and fits:
        return by_kernel(sizes, views, *rest)
    return by_collectives(views, *rest)


def solution(mesh):
    sizes = (mesh.shape["tok"], mesh.shape["grp"], mesh.shape["head"])
    placed = (
        P("grp", None, "tok", None),
        P(None, "head"),
        P(None, "head"),
        P(None, "head"),
        P(None, "head"),
        P("head", None, "tok"),
        P("head", None, "tok"),
        P("head"),
    )
    return jax.shard_map(
        functools.partial(local, sizes), mesh=mesh, in_specs=placed, out_specs=P("grp", None, "tok", "head"), check_vma=False
    )
```

```python
import functools
import math

import jax
import jax.numpy as jnp
from jax import lax
from jax.experimental import pallas as pl
from jax.experimental.pallas import tpu as pltpu
from jax.sharding import PartitionSpec as P

norm_eps = 1e-06
out_eps = 1e-05
step_coef = 0.3
momentum_keep = 0.5


def spread(value, axis, source):
    kept = jnp.where(lax.axis_index(axis) == source, value, 0).astype(value.dtype)
    return lax.psum(kept, axis)


def rms_scale(values):
    return values * lax.rsqrt(jnp.mean(values * values, axis=-1, keepdims=True) + norm_eps)


def contract_rows(left, right):
    return lax.dot_general(
        left, right, (((0,), (0,)), ((), ())), preferred_element_type=jnp.float32
    )


def contract_cols(left, right):
    return lax.dot_general(
        left, right, (((1,), (1,)), ((), ())), preferred_element_type=jnp.float32
    )


def fast_apply(queries, copy_in, copy_out):
    hidden_units = copy_out.shape[0]
    pre_act = jnp.dot(queries, copy_in, preferred_element_type=jnp.float32)
    gate = pre_act[:, :hidden_units]
    upper = pre_act[:, hidden_units:]
    hidden = (gate * jax.nn.sigmoid(gate) * upper).astype(jnp.bfloat16)
    return jnp.dot(hidden, copy_out, preferred_element_type=jnp.float32)


def by_collectives(views, q_weight, k_weight, v_weight, rate_weight, fast_in, fast_out, out_gain):
    tok_count = lax.axis_size("tok")
    is_input = lax.axis_index("grp") == 0
    spans = views.shape[1]
    head_size = fast_in.shape[1]
    hidden_units = fast_out.shape[1]
    step_size = step_coef / math.sqrt(views.shape[2] * tok_count)
    width_all = head_size * lax.axis_size("head")
    whole_in, whole_out = (
        lax.all_gather(fast_in, "tok", axis=2, tiled=True),
        lax.all_gather(fast_out, "tok", axis=2, tiled=True),
    )
    whole_in = whole_in[0]
    whole_out = whole_out[0]
    copy_in = whole_in.astype(jnp.bfloat16)
    copy_out = whole_out.astype(jnp.bfloat16)
    state_in = fast_in[0]
    state_out = fast_out[0]
    base_in = jnp.mean(state_in * state_in, axis=0, keepdims=True)
    base_out = jnp.mean(state_out * state_out, axis=0, keepdims=True)
    moment_in = jnp.zeros_like(state_in)
    moment_out = jnp.zeros_like(state_out)

    def input_grads(inputs, given_in, given_out):
        keyed = rms_scale(jnp.dot(inputs, k_weight, preferred_element_type=jnp.float32)).astype(
            jnp.bfloat16
        )
        valued = jnp.dot(inputs, v_weight, preferred_element_type=jnp.float32)
        rates = jax.nn.softplus(jnp.dot(inputs, rate_weight, preferred_element_type=jnp.float32))
        upstream = (-(step_size * rates) * valued).astype(jnp.bfloat16)
        pre_act = jnp.dot(keyed, given_in, preferred_element_type=jnp.float32)
        gate = pre_act[:, :hidden_units]
        upper = pre_act[:, hidden_units:]
        sigma = jax.nn.sigmoid(gate)
        active = gate * sigma
        hidden = (active * upper).astype(jnp.bfloat16)
        grad_out = contract_rows(hidden, upstream)
        back = contract_cols(upstream, given_out)
        back_pre = jnp.concatenate(
            [back * upper * sigma * (1.0 + gate * (1.0 - sigma)), back * active], axis=1
        ).astype(jnp.bfloat16)
        grad_in = contract_rows(keyed, back_pre)
        return (grad_in, grad_out)

    def novel_grads(inputs, given_in, given_out):
        return (
            jnp.zeros((head_size, 2 * hidden_units), jnp.float32),
            jnp.zeros((hidden_units, head_size), jnp.float32),
        )

    outputs = []
    for span in range(spans):
        inputs = views[0, span]
        queries = rms_scale(jnp.dot(inputs, q_weight, preferred_element_type=jnp.float32)).astype(
            jnp.bfloat16
        )
        grads = lax.cond(is_input, input_grads, novel_grads, inputs, copy_in, copy_out)
        grad_in, grad_out = lax.psum_scatter(grads, "tok", scatter_dimension=1, tiled=True)
        moment_in = momentum_keep * moment_in + grad_in
        moment_out = momentum_keep * moment_out + grad_out
        trial_in = state_in - moment_in
        trial_out = state_out - moment_out
        mean_in = jnp.mean(trial_in * trial_in, axis=0, keepdims=True)
        mean_out = jnp.mean(trial_out * trial_out, axis=0, keepdims=True)
        state_in = trial_in * jnp.sqrt(base_in) * lax.rsqrt(mean_in + norm_eps)
        state_out = trial_out * jnp.sqrt(base_out) * lax.rsqrt(mean_out + norm_eps)
        part_in = state_in.astype(jnp.bfloat16)
        part_out = state_out.astype(jnp.bfloat16)
        copy_in, copy_out = (
            lax.all_gather(part_in, "tok", axis=1, tiled=True),
            lax.all_gather(part_out, "tok", axis=1, tiled=True),
        )
        copy_in, copy_out = (spread(copy_in, "grp", 0), spread(copy_out, "grp", 0))
        produced = fast_apply(queries, copy_in, copy_out)
        squares = lax.psum(jnp.sum(produced * produced, axis=1), "head")
        normed = produced * lax.rsqrt(squares / width_all + out_eps)[:, None] * out_gain
        outputs.append(normed.astype(jnp.bfloat16))
    return jnp.stack(outputs)[None]


def fused_kernel(
    tok_count, grp_count, head_count,
    views_ref, q_ref, k_ref, v_ref, rate_ref, in_ref, out_ref, gain_ref,
    res_ref,
    pieces, packed, queries, keys, ups, moment_in, moment_out, state_in, state_out, copy_in, copy_out,
    base_in, base_out, produced, squares,
    local_sem,
    first_send, first_recv, z_send, z_recv, x_send, x_recv, y_send, y_recv,
    c1_send, c1_recv, c2_send, c2_recv, wz_send, wz_recv, wx_send, wx_recv, sq_send, sq_recv,
):
    tok, grp, head = lax.axis_index("tok"), lax.axis_index("grp"), lax.axis_index("head")
    spans, rows, width = views_ref.shape[1:]
    piece = pieces.shape[-1]
    head_size, block_in = in_ref.shape[1:]
    block_out, hidden_units = out_ref.shape[1:]
    fold = packed.shape[-1] - block_in
    folds = hidden_units // fold
    half = head_size // grp_count
    step_size = step_coef / math.sqrt(rows * tok_count)
    other_grp = {"grp": 1 - grp}
    far_bit = head_count // 2
    far_head = jnp.where(head < far_bit, head + far_bit, head - far_bit)
    flip = 1 - 2 * lax.rem(head, 2)
    near_head = head + flip
    far = {"head": far_head}
    near = {"head": near_head}

    def shard(step):
        return lax.rem(tok - step + tok_count, tok_count)

    def peer(step):
        return {"tok": lax.rem(tok + step, tok_count)}

    def remote(src, dst, send, recv, target):
        return pltpu.make_async_remote_copy(
            src_ref=src, dst_ref=dst, send_sem=send, recv_sem=recv,
            device_id=target, device_id_type=pl.DeviceIdType.MESH,
        )

    def view_piece(span, part):
        start = pl.multiple_of((head * grp_count + part) * piece, piece)
        return views_ref.at[0, span, :, pl.ds(start, piece)]

    def same(ref, send, recv, target):
        return remote(ref, ref, send, recv, target)

    own = [
        pltpu.make_async_copy(view_piece(s, 0), pieces.at[s, tok, head, 0], local_sem.at[s])
        for s in range(spans)
    ]
    first = [
        remote(view_piece(s, 1), pieces.at[s, tok, head, 1], first_send.at[s], first_recv.at[s], other_grp)
        for s in range(spans)
    ]
    along_z = [
        [
            same(pieces.at[s, tok, head, grp], z_send.at[s, d], z_recv.at[s, d], peer(d + 1))
            for d in range(tok_count - 1)
        ]
        for s in range(spans)
    ]
    along_x = [
        [
            same(pieces.at[s, shard(d), head, grp], x_send.at[s, d], x_recv.at[s, d], other_grp)
            for d in range(tok_count)
        ]
        for s in range(spans)
    ]
    along_y = [
        [
            same(pieces.at[s, shard(d), head], y_send.at[s, d], y_recv.at[s, d], far)
            for d in range(tok_count)
        ]
        for s in range(spans)
    ]
    core_own = [
        [
            same(pieces.at[s, shard(d), head], c1_send.at[s, d], c1_recv.at[s, d], near)
            for d in range(tok_count)
        ]
        for s in range(spans)
    ]
    core_far = [
        [
            same(pieces.at[s, shard(d), far_head], c2_send.at[s, d], c2_recv.at[s, d], near)
            for d in range(tok_count)
        ]
        for s in range(spans)
    ]
    my_half = pl.ds(pl.multiple_of(grp * half, half), half)
    fast_z = [
        same(packed.at[tok, my_half], wz_send.at[d], wz_recv.at[d], peer(d + 1))
        for d in range(tok_count - 1)
    ]
    fast_x = [
        same(packed.at[shard(d + 1), my_half], wx_send.at[d], wx_recv.at[d], other_grp)
        for d in range(tok_count - 1)
    ]
    square = [
        [
            same(squares.at[s, head], sq_send.at[s, d], sq_recv.at[s, d],
                 {"head": lax.rem(head + d + 1, head_count)})
            for d in range(head_count - 1)
        ]
        for s in range(spans)
    ]

    barrier = pltpu.get_barrier_semaphore()
    partners = [peer(d + 1) for d in range(tok_count - 1)] + [other_grp]
    partners += [{"head": lax.rem(head + d + 1, head_count)} for d in range(head_count - 1)]
    for target in partners:
        pl.semaphore_signal(barrier, inc=1, device_id=target, device_id_type=pl.DeviceIdType.MESH)

    @pl.when(grp == 0)
    def _():
        for copy in own:
            copy.start()

    packed[tok, :, :block_in] = in_ref[0].astype(jnp.bfloat16)
    for f in range(folds):
        packed[tok, f * block_out:(f + 1) * block_out, block_in:] = out_ref[
            0, :, f * fold:(f + 1) * fold
        ].astype(jnp.bfloat16)
    pl.semaphore_wait(barrier, len(partners))

    @pl.when(grp == 0)
    def _():
        for s in range(spans):
            first[s].start()
        for copy in own:
            copy.wait()
        for copy in along_z[0]:
            copy.start()

    @pl.when(grp == 1)
    def _():
        first[0].wait_recv()
        for copy in along_z[0]:
            copy.start()

    along_x[0][0].start()

    @pl.when(grp == 1)
    def _():
        for s in range(1, spans):
            first[s].wait_recv()

    for s in range(1, spans):
        along_x[s][0].start()
        for copy in along_z[s]:
            copy.start()
    for copy in fast_z:
        copy.start()

    def project_queries(span):
        queries[span] = rms_scale(
            jnp.dot(views_ref[0, span], q_ref[...], preferred_element_type=jnp.float32)
        ).astype(jnp.bfloat16)

    def project(span, t):
        inputs = jnp.concatenate(
            [pieces[span, t, h, g] for h in range(head_count) for g in range(grp_count)], axis=1
        )
        keys[span, t] = rms_scale(
            jnp.dot(inputs, k_ref[...], preferred_element_type=jnp.float32)
        ).astype(jnp.bfloat16)
        valued = jnp.dot(inputs, v_ref[...], preferred_element_type=jnp.float32)
        raw = contract_cols(inputs, jnp.broadcast_to(rate_ref[...], (8, width)))[:, :1]
        rates = jnp.maximum(raw, 0.0) + jnp.log1p(jnp.exp(-jnp.abs(raw)))
        ups[span, t] = (-(step_size * rates) * valued).astype(jnp.bfloat16)

    def forward(span, step):
        if 1 <= step - 1 < tok_count:
            along_x[span][step - 1].wait_recv()
            along_y[span][step - 1].start()
            core_own[span][step - 1].start()
        if 0 <= step - 2 < tok_count:
            along_y[span][step - 2].wait_recv()
            core_far[span][step - 2].start()
        if 0 <= step - 3 < tok_count:
            core_own[span][step - 3].wait_recv()
            core_far[span][step - 3].wait_recv()
            project(span, shard(step - 3))

    def pass_on(span, step):
        along_z[span][step - 1].wait_recv()
        along_x[span][step].start()

    last_step = tok_count + 2
    for s in range(spans):
        along_x[s][0].wait_recv()
        along_y[s][0].start()
        core_own[s][0].start()
    project_queries(0)
    for step in range(1, last_step + 1):
        if step < tok_count:
            pass_on(0, step)
        forward(0, step)
        for s in range(1, spans):
            if 0 <= step - tok_count < tok_count - 1:
                pass_on(s, step - tok_count + 1)
    for d in range(tok_count - 1):
        fast_z[d].wait_recv()
        fast_x[d].start()
    for s in range(1, spans):
        for step in range(1, tok_count + 1):
            forward(s, step)
    for s in range(1, spans):
        project_queries(s)
    for d in range(tok_count - 1):
        fast_x[d].wait_recv()

    for t in range(tok_count):
        cols = slice(t * block_in, (t + 1) * block_in)
        given = packed[t, :, :block_in]
        wide = given.astype(jnp.float32)
        copy_in[:, cols] = given
        state_in[:, cols] = wide
        base_in[:, cols] = jnp.sqrt(jnp.mean(wide * wide, axis=0, keepdims=True))
        for f in range(folds):
            part = slice(f * fold, (f + 1) * fold)
            turned = slice(t * block_out, (t + 1) * block_out)
            given = packed[t, f * block_out:(f + 1) * block_out, block_in:]
            copy_out[turned, part] = given
            state_out[turned, part] = given.astype(jnp.float32)
    base_out[...] = jnp.sqrt(jnp.mean(state_out[...] * state_out[...], axis=1, keepdims=True))
    moment_in[...] = jnp.zeros_like(moment_in)
    moment_out[...] = jnp.zeros_like(moment_out)

    def add_grads(span, t):
        keyed, upstream = keys[span, t], ups[span, t]
        gate = jnp.dot(keyed, copy_in[:, :hidden_units], preferred_element_type=jnp.float32)
        upper = jnp.dot(keyed, copy_in[:, hidden_units:], preferred_element_type=jnp.float32)
        sigma = jax.nn.sigmoid(gate)
        active = gate * sigma
        hidden = (active * upper).astype(jnp.bfloat16)
        moment_out[...] += contract_rows(upstream, hidden)
        back = jnp.dot(upstream, copy_out[...], preferred_element_type=jnp.float32)
        back_gate = (back * upper * sigma * (1.0 + gate * (1.0 - sigma))).astype(jnp.bfloat16)
        back_upper = (back * active).astype(jnp.bfloat16)
        moment_in[:, :hidden_units] += contract_rows(keyed, back_gate)
        moment_in[:, hidden_units:] += contract_rows(keyed, back_upper)

    def renormalize(state, moment, base, axis):
        trial = state - moment
        mean = jnp.mean(trial * trial, axis=axis, keepdims=True)
        return trial * base * lax.rsqrt(mean + norm_eps)

    for s in range(spans):
        for d in range(tok_count):
            add_grads(s, d)
            if s + 1 < spans:
                if tok_count + 1 + d <= last_step:
                    forward(s + 1, tok_count + 1 + d)
        for t in range(tok_count):
            cols = slice(t * block_in, (t + 1) * block_in)
            fresh = renormalize(state_in[:, cols], moment_in[:, cols], base_in[:, cols], 0)
            copy_in[:, cols] = fresh.astype(jnp.bfloat16)
            if s + 1 < spans:
                state_in[:, cols] = fresh
                moment_in[:, cols] *= momentum_keep
            turned = slice(t * block_out, (t + 1) * block_out)
            fresh = renormalize(state_out[turned], moment_out[turned], base_out[turned], 1)
            copy_out[turned] = fresh.astype(jnp.bfloat16)
            if s + 1 < spans:
                state_out[turned] = fresh
                moment_out[turned] *= momentum_keep
        pre_act = jnp.dot(queries[s], copy_in[...], preferred_element_type=jnp.float32)
        gate = pre_act[:, :hidden_units]
        hidden = (gate * jax.nn.sigmoid(gate) * pre_act[:, hidden_units:]).astype(jnp.bfloat16)
        made = contract_cols(hidden, copy_out[...])
        produced[s] = made
        sums = jnp.sum(made * made, axis=1, keepdims=True)
        squares[s, head] = jnp.transpose(jnp.broadcast_to(sums, (rows, 128)))[:8]
        for copy in square[s]:
            copy.start()

    for s in range(spans):
        for copy in square[s]:
            copy.wait_recv()
        total = squares[s, 0]
        for h in range(1, head_count):
            total = total + squares[s, h]
        scale = lax.rsqrt(total / (head_size * head_count) + out_eps)
        column = jnp.transpose(jnp.concatenate([scale] * 16, axis=0))[:, :1]
        res_ref[0, s] = (produced[s] * column * gain_ref[...]).astype(jnp.bfloat16)

    @pl.when(grp == 0)
    def _():
        for copy in first:
            copy.wait_send()

    for group in (along_z, along_x, along_y, core_own, core_far, square):
        for copies in group:
            for copy in copies:
                copy.wait_send()
    for copy in fast_z + fast_x:
        copy.wait_send()


def by_kernel(sizes, views, q_weight, k_weight, v_weight, rate_weight, fast_in, fast_out, out_gain):
    tok_count, grp_count, head_count = sizes
    _, spans, rows, width = views.shape
    _, head_size, block_in = fast_in.shape
    _, hidden_units, block_out = fast_out.shape
    piece = width // (grp_count * head_count)
    fold = hidden_units * block_out // head_size
    dma = pltpu.SemaphoreType.DMA
    vmem = pltpu.VMEM
    pair = [dma((spans, tok_count))] * 2
    return pl.pallas_call(
        functools.partial(fused_kernel, tok_count, grp_count, head_count),
        out_shape=jax.ShapeDtypeStruct((1, spans, rows, head_size), jnp.bfloat16),
        in_specs=[pl.BlockSpec(memory_space=pltpu.VMEM)] * 8,
        out_specs=pl.BlockSpec(memory_space=pltpu.VMEM),
        scratch_shapes=[
            vmem((spans, tok_count, head_count, grp_count, rows, piece), jnp.bfloat16),
            vmem((tok_count, head_size, block_in + fold), jnp.bfloat16),
            vmem((spans, rows, head_size), jnp.bfloat16),
            vmem((spans, tok_count, rows, head_size), jnp.bfloat16),
            vmem((spans, tok_count, rows, head_size), jnp.bfloat16),
            vmem((head_size, 2 * hidden_units), jnp.float32),
            vmem((head_size, hidden_units), jnp.float32),
            vmem((head_size, 2 * hidden_units), jnp.float32),
            vmem((head_size, hidden_units), jnp.float32),
            vmem((head_size, 2 * hidden_units), jnp.bfloat16),
            vmem((head_size, hidden_units), jnp.bfloat16),
            vmem((1, 2 * hidden_units), jnp.float32),
            vmem((head_size, 1), jnp.float32),
            vmem((spans, rows, head_size), jnp.float32),
            vmem((spans, head_count, 8, rows), jnp.float32),
            dma((spans,)),
            *[dma((spans,))] * 2,
            *[dma((spans, tok_count - 1))] * 2,
            *pair, *pair, *pair, *pair,
            *[dma((tok_count - 1,))] * 4,
            *[dma((spans, head_count - 1))] * 2,
        ],
        compiler_params=pltpu.CompilerParams(collective_id=0, has_side_effects=True),
        name="fused_layer",
    )(
        views, q_weight, k_weight, v_weight, rate_weight.T, fast_in,
        jnp.swapaxes(fast_out, 1, 2), out_gain.reshape(1, -1),
    )


def local(sizes, views, *rest):
    tok_count, grp_count, head_count = sizes
    fast_in, fast_out = rest[4], rest[5]
    head_size, hidden_units = fast_in.shape[1], fast_out.shape[1]
    piece = views.shape[3] // (grp_count * head_count)
    few = tok_count * views.shape[2] <= 4 * head_size
    fits = (
        tok_count > 1 and grp_count == 2 and head_count == 4 and piece % 128 == 0
        and fast_in.shape[2] % 128 == 0 and views.shape[2] % 16 == 0 and head_size % fast_out.shape[2] == 0
        and fast_out.shape[2] * hidden_units % (128 * head_size) == 0 and fast_out.shape[2] % 16 == 0
    )
    if few and fits:
        return by_kernel(sizes, views, *rest)
    return by_collectives(views, *rest)


def solution(mesh):
    sizes = (mesh.shape["tok"], mesh.shape["grp"], mesh.shape["head"])
    placed = (
        P("grp", None, "tok", None),
        P(None, "head"),
        P(None, "head"),
        P(None, "head"),
        P(None, "head"),
        P("head", None, "tok"),
        P("head", None, "tok"),
        P("head"),
    )
    return jax.shard_map(
        functools.partial(local, sizes), mesh=mesh, in_specs=placed, out_specs=P("grp", None, "tok", "head"), check_vma=False
    )
```
